512 devices in a mesh: gx: 8 (over x, core), gy: 8 (over z), gz: 8 (over y).
Axes of the slice: x: 4, y: 8, z: 8, core: 2. Of those that a mesh axis runs over, the one named last changes fastest.
Arguments:
- outcomes: bfloat16 [393216, 2048], P(('gx', 'gy', 'gz')), may hold values from -6 to 6
- sketch: bfloat16 [393216, 128], P(('gx', 'gy', 'gz')), may hold values from -6 to 6
Outputs:
- left_basis: float32 [393216, 128], P(('gx', 'gy', 'gz'))
- factor: float32 [128, 128], replicated
The draws below stay inside these ranges and needn't reach their ends.
All inputs are finite; a program needn't handle non-finite values.
Results may differ from the reference program's by a relative error of at most 0.005.
Values may be sent and summed in bfloat16 or wider, within the bound.
No kernel may reach another device: no remote copies, remote signals or barrier semaphores. Data moves between devices by JAX's collectives and lax.ppermute only.
A program may use at most 64 MiB of HBM per device.

```python
import math
import jax
import jax.numpy as jnp
from jax import lax

DAYS = 2048
RANK = 128
POWER = 2
UNITS = 393216


def block_scale(own_key, extent, pieces, smallest, high):
    def one(axis_at, blocks):
        heights = jax.random.uniform(jax.random.fold_in(jax.random.fold_in(own_key, 6), axis_at), (blocks,), jnp.float32, smallest / len(pieces), high / len(pieces))
        return jnp.repeat(jnp.exp(heights), extent[axis_at] // blocks).reshape((-1,) + (1,) * (len(extent) - axis_at - 1))

    level = one(*pieces[0])
    for cut in pieces[1:]:
        level = level * one(*cut)
    return level


def centred(own_key, dims, spread, reach, split=(), dtype=jnp.bfloat16):
    gain = block_scale(own_key, dims, split, -0.22, 0.18) if split else 1.0
    drawn = jax.random.normal(own_key, dims, jnp.float32) * spread * gain
    return jnp.minimum(jnp.maximum(drawn, -reach), reach).astype(dtype)


def setup_inputs(seed: int = 0) -> dict:
    splits = jax.random.split(jax.random.key(seed), 3)
    return {
        "outcomes": centred(splits[0], (UNITS, DAYS), 1.0, 6.0, ((0, 512),)),
        "sketch": centred(splits[1], (UNITS, RANK), 1.0, 6.0, ((0, 512),)),
    }


def reference(outcomes, sketch):
    current = sketch
    left_basis = None
    factor = None
    for power_step in range(POWER):
        summed = lax.dot_general(outcomes.astype(jnp.float32), current.astype(jnp.float32), (((0,), (0,)), ((), ())), preferred_element_type=jnp.float32)
        day_weights = (summed / math.sqrt(UNITS)).astype(jnp.bfloat16)
        projected = jnp.dot(outcomes.astype(jnp.float32), day_weights.astype(jnp.float32), preferred_element_type=jnp.float32) / math.sqrt(DAYS)
        gram = jnp.dot(projected.T, projected, precision=lax.Precision.HIGHEST) / UNITS
        lower_tri = jnp.linalg.cholesky(gram)
        left_basis = lax.linalg.triangular_solve(lower_tri, projected, left_side=False, lower=True, transpose_a=True)
        factor = lower_tri.T
        current = left_basis.astype(jnp.bfloat16)
    return (left_basis, factor)
```

```python
import math

import jax
import jax.numpy as jnp
from jax import lax
from jax.sharding import Mesh
from jax.sharding import PartitionSpec as P

X, C, Z, Y = "gx_0", "gx_1", "gy", "gz"
EVERY = (X, C, Z, Y)
F32, BF16 = jnp.float32, jnp.bfloat16
HIGHEST = lax.Precision.HIGHEST


def swap(block):
    return lax.ppermute(block, C, [(0, 1), (1, 0)])


def exchange(blocks, axes):
    return lax.all_to_all(blocks, axes, split_axis=0, concat_axis=0, tiled=True)


def to_all(block, axes):
    copies = jnp.broadcast_to(block, (lax.axis_size(axes), *block.shape))
    return exchange(copies, axes)


def own_half(whole):
    half = whole.shape[0] // 2
    core = lax.axis_index(C)
    mine = lax.dynamic_slice_in_dim(whole, core * half, half, 0)
    other = lax.dynamic_slice_in_dim(whole, (1 - core) * half, half, 0)
    return mine + swap(other)


def both_halves(mine):
    other = swap(mine)
    first = lax.axis_index(C) == 0
    return jnp.concatenate([jnp.where(first, mine, other), jnp.where(first, other, mine)], 0)


def scattered_sum(part, axes):
    blocks = part.reshape(lax.axis_size(axes), -1, part.shape[-1])
    return exchange(blocks, axes).sum(axis=0)


def gathered(own, axes):
    return to_all(own, axes).reshape(-1, own.shape[-1])


def row_sums(part):
    mine = own_half(part)
    mine = scattered_sum(mine, X)
    return scattered_sum(mine, (Z, Y))


def gram_sum(part):
    mine = scattered_sum(own_half(part), X)
    mine = to_all(mine, Z).sum(axis=0)
    mine = to_all(mine, Y).sum(axis=0)
    return both_halves(gathered(mine, X))


def transposed_dot(rows, columns):
    return lax.dot_general(rows, columns, (((0,), (0,)), ((), ())), preferred_element_type=F32)


def solved(lower, rows):
    return lax.linalg.triangular_solve(lower, rows, left_side=False, lower=True, transpose_a=True)


def per_device(outcomes, sketch):
    rows_here, day_count = outcomes.shape
    rank = sketch.shape[1]
    unit_count = rows_here * lax.axis_size(EVERY)
    per_unit, per_day = 1 / math.sqrt(unit_count), 1 / math.sqrt(day_count)

    own = row_sums(transposed_dot(outcomes, sketch))
    weights = both_halves(gathered((own * per_unit).astype(BF16), (X, Z, Y)))

    projected = jnp.dot(outcomes, weights, preferred_element_type=F32) * per_day
    high = projected.astype(BF16)
    low = (projected - high.astype(F32)).astype(BF16)
    split = transposed_dot(outcomes, jnp.concatenate([high, low], 1))
    own = row_sums(split[:, :rank] + split[:, rank:])
    back = both_halves(gathered(gathered(own, (Z, Y)), X))
    gram = lax.dot_general(
        weights.astype(F32), back, (((0,), (0,)), ((), ())), precision=HIGHEST
    ) * (per_day / unit_count)
    lower = jnp.linalg.cholesky(gram)
    weights = (solved(lower, back) * per_unit).astype(BF16)

    projected = jnp.dot(outcomes, weights, preferred_element_type=F32) * per_day
    gram = gram_sum(jnp.dot(projected.T, projected, precision=HIGHEST) / unit_count)
    lower = jnp.linalg.cholesky(gram)
    return solved(lower, projected), lower.T


def solution(mesh):
    finer = Mesh(
        mesh.devices.reshape(4, 2, mesh.shape["gy"], mesh.shape["gz"]), EVERY
    )
    return jax.shard_map(
        per_device,
        mesh=finer,
        in_specs=(P(EVERY, None), P(EVERY, None)),
        out_specs=(P(EVERY, None), P()),
        check_vma=False,
    )
```

```python
import functools
import math

import jax
import jax.numpy as jnp
from jax import lax
from jax.experimental import pallas as pl
from jax.experimental.pallas import tpu as pltpu
from jax.sharding import Mesh
from jax.sharding import PartitionSpec as P

X, C, Z, Y = "gx_0", "gx_1", "gy", "gz"
EVERY = (X, C, Z, Y)
F32, BF16 = jnp.float32, jnp.bfloat16

LANES, SUBLANES, BLOCK = 128, 8, 32


def full(value):
    return jnp.broadcast_to(value, (SUBLANES, LANES))


def reciprocal(value):
    guess = pltpu.reciprocal(value, approx=True)
    guess = guess * (2.0 - value * guess)
    return guess * (2.0 - value * guess)


def inverse_root(value):
    guess = lax.rsqrt(value)
    return guess * (1.5 - 0.5 * value * guess * guess)


def three_terms(value):
    high = value.astype(BF16)
    rest = value - high.astype(F32)
    middle = rest.astype(BF16)
    return high, middle, (rest - middle.astype(F32)).astype(BF16)


def bf16_dot(left, right, dims):
    return lax.dot_general(left, right, (dims, ((), ())), preferred_element_type=F32)


FIRSTS, LASTS = ((0,), (0,)), ((1,), (1,))


def self_product(value):
    terms = [term.astype(F32) for term in three_terms(value)]
    left = jnp.concatenate([terms[i] for i in (0, 0, 1, 0, 2, 1)], 0).astype(BF16)
    right = jnp.concatenate([terms[i] for i in (0, 1, 0, 2, 0, 1)], 0).astype(BF16)
    return bf16_dot(left, right, FIRSTS)


def eliminated(rows, start, lane, sub):
    groups = len(rows)
    count = SUBLANES * groups
    columns = [
        [full(rows[v][:, start + m : start + m + 1]) if v >= m // 8 else None for v in range(groups)]
        for m in range(count)
    ]
    inside = (lane >= start) & (lane < start + count)
    solved_rows = [
        jnp.where(inside, jnp.where(lane - start - 8 * v == sub, 1.0, 0.0), rows[v])
        for v in range(groups)
    ]
    upper = list(rows)
    pivots = [None] * groups
    for j in range(count):
        at, s = divmod(j, SUBLANES)
        pivot = full(columns[j][at][s : s + 1, :])
        pivots[at] = pivot if s == 0 else jnp.where(sub == s, pivot, pivots[at])
        if j == count - 1:
            break
        scale = reciprocal(pivot)
        steps = {v: columns[j][v] * scale for v in range(at, groups)}
        steps[at] = jnp.where(sub > s, steps[at], 0.0)
        for m in range(j + 1, count):
            entry = full(columns[j][m // 8][m % 8 : m % 8 + 1, :])
            for v in range(m // 8, groups):
                columns[m][v] = columns[m][v] - steps[v] * entry
        for held in (solved_rows, upper):
            row = full(held[at][s : s + 1, :])
            for v in range(at, groups):
                held[v] = held[v] - steps[v] * row
    for v in range(groups):
        root = inverse_root(pivots[v])
        solved_rows[v] = solved_rows[v] * root
        upper[v] = jnp.where(lane >= start + 8 * v + sub, upper[v] * root, 0.0)
    return solved_rows, upper, inside


def factored(gram):
    lane = lax.broadcasted_iota(jnp.int32, (SUBLANES, LANES), 1)
    sub = lax.broadcasted_iota(jnp.int32, (SUBLANES, LANES), 0)
    total, groups = gram.shape[0] // SUBLANES, BLOCK // SUBLANES
    left = [gram[8 * v : 8 * v + 8, :] for v in range(total)]
    inverse, factor = [], []
    for k in range(0, total, groups):
        rows, upper, inside = eliminated(left[k : k + groups], SUBLANES * k, lane, sub)
        factor += upper
        inverse += [jnp.where(lane <= 8 * (k + v) + sub, rows[v], 0.0) for v in range(groups)]
        if k + groups < total:
            update = self_product(jnp.concatenate(rows, 0))
            for v in range(k + groups, total):
                left[v] = jnp.where(inside, 0.0, left[v]) - update[8 * v : 8 * v + 8, :]
    return jnp.concatenate(inverse, 0), jnp.concatenate(factor, 0)


def times_transposed(rows, matrix):
    high, middle, low = three_terms(matrix)
    left = jnp.concatenate([rows[i] for i in (0, 0, 1, 0, 2, 1)], 1)
    right = jnp.concatenate([high, middle, high, low, high, middle], 1)
    return bf16_dot(left, right, LASTS)


def middle_kernel(
    scales, core, outcomes, weights_mine, weights_other, back_mine, back_other,
    projected, gram_mine, gram_other, panel, copied,
):
    per_unit, per_day, gram_scale, last_scale = scales
    fetch = pltpu.make_async_copy(outcomes, panel, copied)
    fetch.start()
    half = back_mine.shape[0]
    gram = jnp.zeros((LANES, LANES), F32)
    terms = []
    for weights, back in ((weights_mine, back_mine), (weights_other, back_other)):
        split = three_terms(back[...])
        terms.append(split)
        product = bf16_dot(weights[...], jnp.concatenate(split, 1), FIRSTS)
        for i in range(3):
            gram += product[:, LANES * i : LANES * (i + 1)]
    inverse, _ = factored(gram * gram_scale)
    fresh = [(times_transposed(split, inverse) * per_unit).astype(BF16) for split in terms]
    fetch.wait()
    result = jnp.zeros(projected.shape, F32)
    for i, part in enumerate(fresh):
        side = core[0] if i == 0 else 1 - core[0]
        days = panel[:, pl.ds(pl.multiple_of(side * half, half), half)]
        result += jnp.dot(days, part, preferred_element_type=F32)
    result = result * per_day
    projected[...] = result
    high, middle, low = three_terms(result)
    product = bf16_dot(high, jnp.concatenate([high, middle, low], 1), FIRSTS)
    cross = product[:, LANES : 2 * LANES] + product[:, 2 * LANES :]
    total = product[:, :LANES] + bf16_dot(middle, middle, FIRSTS) + cross + cross.T
    total = total * last_scale
    first = core[0] == 0
    top, bottom = total[: LANES // 2], total[LANES // 2 :]
    gram_mine[...] = jnp.where(first, top, bottom)
    gram_other[...] = jnp.where(first, bottom, top)


def last_kernel(core, gram_mine, gram_other, projected, basis, factor):
    first = core[0] == 0
    mine, other = gram_mine[...], gram_other[...]
    gram = jnp.concatenate([jnp.where(first, mine, other), jnp.where(first, other, mine)], 0)
    inverse, upper = factored(gram)
    factor[...] = upper
    basis[...] = times_transposed(three_terms(projected[...]), inverse)


def specs(*spaces):
    return [pl.BlockSpec(memory_space=space) for space in spaces]


def shapes(*dims):
    return [jax.ShapeDtypeStruct(dim, F32) for dim in dims]


VMEM, SMEM, ANY = pltpu.VMEM, pltpu.SMEM, pl.ANY


def middle_stage(core, outcomes, weights, back, scales):
    rows, rank = outcomes.shape[0], back[0].shape[1]
    return pl.pallas_call(
        functools.partial(middle_kernel, scales),
        out_shape=shapes((rows, rank), (rank // 2, rank), (rank // 2, rank)),
        in_specs=specs(SMEM, ANY, VMEM, VMEM, VMEM, VMEM),
        out_specs=specs(VMEM, VMEM, VMEM),
        scratch_shapes=[pltpu.VMEM(outcomes.shape, BF16), pltpu.SemaphoreType.DMA],
        compiler_params=pltpu.CompilerParams(vmem_limit_bytes=32 << 20),
        name="middle_stage",
    )(core, outcomes, *weights, *back)


def last_stage(core, gram, projected):
    rank = projected.shape[1]
    return pl.pallas_call(
        last_kernel,
        out_shape=shapes(projected.shape, (rank, rank)),
        in_specs=specs(SMEM, VMEM, VMEM, VMEM),
        out_specs=specs(VMEM, VMEM),
        compiler_params=pltpu.CompilerParams(vmem_limit_bytes=16 << 20),
        name="last_stage",
    )(core, *gram, projected)


def swap(block):
    return lax.ppermute(block, C, [(0, 1), (1, 0)])


def exchange(blocks, axes):
    return lax.all_to_all(blocks, axes, split_axis=0, concat_axis=0, tiled=True)


def to_all(block, axes):
    copies = jnp.broadcast_to(block, (lax.axis_size(axes), *block.shape))
    return exchange(copies, axes)


def own_half(whole):
    half = whole.shape[0] // 2
    core = lax.axis_index(C)
    mine = lax.dynamic_slice_in_dim(whole, core * half, half, 0)
    other = lax.dynamic_slice_in_dim(whole, (1 - core) * half, half, 0)
    return mine + swap(other)


def scattered_sum(part, axes):
    blocks = part.reshape(lax.axis_size(axes), -1, part.shape[-1])
    return exchange(blocks, axes).sum(axis=0)


def gathered(own, axes):
    return to_all(own, axes).reshape(-1, own.shape[-1])


def row_sums(part):
    mine = own_half(part)
    mine = scattered_sum(mine, X)
    return scattered_sum(mine, (Z, Y))


def gram_sum(mine, other):
    mine = scattered_sum(mine + swap(other), X)
    mine = to_all(mine, Z).sum(axis=0)
    mine = to_all(mine, Y).sum(axis=0)
    mine = gathered(mine, X)
    return mine, swap(mine)


def transposed_dot(rows, columns):
    return lax.dot_general(rows, columns, (FIRSTS, ((), ())), preferred_element_type=F32)


def per_device(outcomes, sketch):
    rows_here, day_count = outcomes.shape
    rank = sketch.shape[1]
    unit_count = rows_here * lax.axis_size(EVERY)
    per_unit, per_day = 1 / math.sqrt(unit_count), 1 / math.sqrt(day_count)
    core = lax.axis_index(C).astype(jnp.int32).reshape(1)

    own = row_sums(transposed_dot(outcomes, sketch))
    mine = gathered((own * per_unit).astype(BF16), (X, Z, Y))
    other = swap(mine)
    first = lax.axis_index(C) == 0
    weights = jnp.concatenate([jnp.where(first, mine, other), jnp.where(first, other, mine)], 0)

    projected = jnp.dot(outcomes, weights, preferred_element_type=F32) * per_day
    high = projected.astype(BF16)
    low = (projected - high.astype(F32)).astype(BF16)
    split = transposed_dot(outcomes, jnp.concatenate([high, low], 1))
    own = row_sums(split[:, :rank] + split[:, rank:])
    back = gathered(gathered(own, (Z, Y)), X)
    scales = (per_unit, per_day, per_day / unit_count, 1 / unit_count)
    projected, *halves = middle_stage(core, outcomes, (mine, other), (back, swap(back)), scales)
    return tuple(last_stage(core, gram_sum(*halves), projected))


def solution(mesh):
    finer = Mesh(
        mesh.devices.reshape(4, 2, mesh.shape["gy"], mesh.shape["gz"]), EVERY
    )
    return jax.shard_map(
        per_device,
        mesh=finer,
        in_specs=(P(EVERY, None), P(EVERY, None)),
        out_specs=(P(EVERY, None), P()),
        check_vma=False,
    )
```

```python
import functools
import math

import jax
import jax.numpy as jnp
from jax import lax
from jax.experimental import pallas as pl
from jax.experimental.pallas import tpu as pltpu
from jax.sharding import Mesh
from jax.sharding import PartitionSpec as P

X, C, Z, Y = "gx_0", "gx_1", "gy", "gz"
EVERY = (X, C, Z, Y)
F32, BF16 = jnp.float32, jnp.bfloat16

LANES, SUBLANES, BLOCK, CHUNKS = 128, 8, 32, 3


def full(value):
    return jnp.broadcast_to(value, (SUBLANES, LANES))


def reciprocal(value):
    guess = pltpu.reciprocal(value, approx=True)
    guess = guess * (2.0 - value * guess)
    return guess * (2.0 - value * guess)


def inverse_root(value):
    guess = lax.rsqrt(value)
    return guess * (1.5 - 0.5 * value * guess * guess)


def three_terms(value):
    high = value.astype(BF16)
    rest = value - high.astype(F32)
    middle = rest.astype(BF16)
    return high, middle, (rest - middle.astype(F32)).astype(BF16)


def bf16_dot(left, right, dims):
    return lax.dot_general(left, right, (dims, ((), ())), preferred_element_type=F32)


FIRSTS, LASTS = ((0,), (0,)), ((1,), (1,))


def self_product(value):
    terms = [term.astype(F32) for term in three_terms(value)]
    left = jnp.concatenate([terms[i] for i in (0, 0, 1, 0, 2, 1)], 0).astype(BF16)
    right = jnp.concatenate([terms[i] for i in (0, 1, 0, 2, 0, 1)], 0).astype(BF16)
    return bf16_dot(left, right, FIRSTS)


def eliminated(rows, start, lane, sub):
    groups = len(rows)
    count = SUBLANES * groups
    columns = [
        [full(rows[v][:, start + m : start + m + 1]) if v >= m // 8 else None for v in range(groups)]
        for m in range(count)
    ]
    inside = (lane >= start) & (lane < start + count)
    solved_rows = [
        jnp.where(inside, jnp.where(lane - start - 8 * v == sub, 1.0, 0.0), rows[v])
        for v in range(groups)
    ]
    upper = list(rows)
    pivots = [None] * groups
    for j in range(count):
        at, s = divmod(j, SUBLANES)
        pivot = full(columns[j][at][s : s + 1, :])
        pivots[at] = pivot if s == 0 else jnp.where(sub == s, pivot, pivots[at])
        if j == count - 1:
            break
        scale = reciprocal(pivot)
        steps = {v: columns[j][v] * scale for v in range(at, groups)}
        steps[at] = jnp.where(sub > s, steps[at], 0.0)
        for m in range(j + 1, count):
            entry = full(columns[j][m // 8][m % 8 : m % 8 + 1, :])
            for v in range(m // 8, groups):
                columns[m][v] = columns[m][v] - steps[v] * entry
        for held in (solved_rows, upper):
            row = full(held[at][s : s + 1, :])
            for v in range(at, groups):
                held[v] = held[v] - steps[v] * row
    for v in range(groups):
        root = inverse_root(pivots[v])
        solved_rows[v] = solved_rows[v] * root
        upper[v] = jnp.where(lane >= start + 8 * v + sub, upper[v] * root, 0.0)
    return solved_rows, upper, inside


def factored(gram):
    lane = lax.broadcasted_iota(jnp.int32, (SUBLANES, LANES), 1)
    sub = lax.broadcasted_iota(jnp.int32, (SUBLANES, LANES), 0)
    total, groups = gram.shape[0] // SUBLANES, BLOCK // SUBLANES
    left = [gram[8 * v : 8 * v + 8, :] for v in range(total)]
    inverse, factor = [], []
    for k in range(0, total, groups):
        rows, upper, inside = eliminated(left[k : k + groups], SUBLANES * k, lane, sub)
        factor += upper
        inverse += [jnp.where(lane <= 8 * (k + v) + sub, rows[v], 0.0) for v in range(groups)]
        if k + groups < total:
            update = self_product(jnp.concatenate(rows, 0))
            for v in range(k + groups, total):
                left[v] = jnp.where(inside, 0.0, left[v]) - update[8 * v : 8 * v + 8, :]
    return jnp.concatenate(inverse, 0), jnp.concatenate(factor, 0)


def times_transposed(rows, matrix):
    high, middle, low = three_terms(matrix)
    left = jnp.concatenate([rows[i] for i in (0, 0, 1, 0, 2, 1)], 1)
    right = jnp.concatenate([high, middle, high, low, high, middle], 1)
    return bf16_dot(left, right, LASTS)


def days_of(panel, side):
    half = panel.shape[1] // 2
    return panel[:, pl.ds(pl.multiple_of(side * half, half), half)]


def first_kernel(core, outcomes, sketch, mine, other, panel, columns, copied):
    rows = outcomes.shape[0] // CHUNKS
    copies = [pltpu.make_async_copy(sketch, columns, copied.at[CHUNKS])]
    for i in range(CHUNKS):
        here = pl.ds(i * rows, rows)
        copies.append(pltpu.make_async_copy(outcomes.at[here], panel.at[here], copied.at[i]))
    for copy in copies:
        copy.start()
    copies[0].wait()
    for i in range(CHUNKS):
        copies[i + 1].wait()
        here = pl.ds(i * rows, rows)
        for out, side in ((other, 1 - core[0]), (mine, core[0])):
            product = bf16_dot(days_of(panel.at[here], side), columns[here, :], FIRSTS)
            out[...] = product if i == 0 else out[...] + product


def projection(outcomes, core, weights_mine, weights_other):
    result = jnp.dot(days_of(outcomes, core[0]), weights_mine, preferred_element_type=F32)
    return result + jnp.dot(
        days_of(outcomes, 1 - core[0]), weights_other, preferred_element_type=F32
    )


def back_kernel(
    per_day, core, outcomes, weights_mine, weights_other, mine, other, panel, copied
):
    rows = outcomes.shape[0] // CHUNKS
    places = [pl.ds(i * rows, rows) for i in range(CHUNKS)]
    copies = [
        pltpu.make_async_copy(outcomes.at[here], panel.at[here], copied.at[i])
        for i, here in enumerate(places)
    ]
    for copy in copies:
        copy.start()
    for i, here in enumerate(places):
        copies[i].wait()
        part = panel.at[here]
        projected = projection(part, core, weights_mine[...], weights_other[...]) * per_day
        high, low, _ = three_terms(projected)
        split = jnp.concatenate([high, low], 1)
        for out, side in ((other, 1 - core[0]), (mine, core[0])):
            product = bf16_dot(days_of(part, side), split, FIRSTS)
            product = product[:, :LANES] + product[:, LANES:]
            out[...] = product if i == 0 else out[...] + product


def middle_kernel(
    scales, core, outcomes, weights_mine, weights_other, back_mine, back_other,
    projected, gram_out, panel, held, copied,
):
    per_unit, per_day, gram_scale, last_scale = scales
    fetch = pltpu.make_async_copy(outcomes, panel, copied.at[0])
    fetch.start()
    gram = jnp.zeros((LANES, LANES), F32)
    terms = []
    for weights, back in ((weights_mine, back_mine), (weights_other, back_other)):
        split = three_terms(back[...])
        terms.append(split)
        product = bf16_dot(weights[...], jnp.concatenate(split, 1), FIRSTS)
        for i in range(3):
            gram += product[:, LANES * i : LANES * (i + 1)]
    inverse, _ = factored(gram * gram_scale)
    fresh = [(times_transposed(split, inverse) * per_unit).astype(BF16) for split in terms]
    fetch.wait()
    result = projection(panel, core, *fresh) * per_day
    held[...] = result
    store = pltpu.make_async_copy(held, projected, copied.at[1])
    store.start()
    high, middle, low = three_terms(result)
    product = bf16_dot(high, jnp.concatenate([high, middle, low], 1), FIRSTS)
    cross = product[:, LANES : 2 * LANES] + product[:, 2 * LANES :]
    total = product[:, :LANES] + bf16_dot(middle, middle, FIRSTS) + cross + cross.T
    gram_out[...] = total * last_scale
    store.wait()


def last_kernel(gram, projected, basis, factor, held, copied):
    fetch = pltpu.make_async_copy(projected, held, copied)
    fetch.start()
    inverse, upper = factored(gram[...])
    factor[...] = upper
    fetch.wait()
    basis[...] = times_transposed(three_terms(held[...]), inverse)


def sum_kernel(blocks, total):
    total[...] = blocks[...].sum(axis=0)


def specs(*spaces):
    return [pl.BlockSpec(memory_space=space) for space in spaces]


VMEM, SMEM, HBM = pltpu.VMEM, pltpu.SMEM, pltpu.HBM


def shapes(*dims):
    return [VMEM(dim, F32) for dim in dims]


def in_hbm(array):
    return pltpu.with_memory_space_constraint(array, HBM)


def first_stage(core, outcomes, sketch):
    half = (outcomes.shape[1] // 2, sketch.shape[1])
    return pl.pallas_call(
        first_kernel,
        out_shape=shapes(half, half),
        in_specs=specs(SMEM, HBM, HBM),
        out_specs=specs(VMEM, VMEM),
        scratch_shapes=[
            pltpu.VMEM(outcomes.shape, BF16),
            pltpu.VMEM(sketch.shape, BF16),
            pltpu.SemaphoreType.DMA((CHUNKS + 1,)),
        ],
        compiler_params=pltpu.CompilerParams(vmem_limit_bytes=16 << 20),
        name="first_stage",
    )(core, in_hbm(outcomes), in_hbm(sketch))


def back_stage(core, outcomes, weights, per_day):
    half = weights[0].shape
    return pl.pallas_call(
        functools.partial(back_kernel, per_day),
        out_shape=shapes(half, half),
        in_specs=specs(SMEM, HBM, VMEM, VMEM),
        out_specs=specs(VMEM, VMEM),
        scratch_shapes=[pltpu.VMEM(outcomes.shape, BF16), pltpu.SemaphoreType.DMA((CHUNKS,))],
        compiler_params=pltpu.CompilerParams(vmem_limit_bytes=24 << 20),
        name="back_stage",
    )(core, in_hbm(outcomes), *weights)


def middle_stage(core, outcomes, weights, back, scales):
    projected = (outcomes.shape[0], back[0].shape[1])
    rank = projected[1]
    return pl.pallas_call(
        functools.partial(middle_kernel, scales),
        out_shape=[pltpu.HBM(projected, F32), pltpu.VMEM((rank, rank), F32)],
        in_specs=specs(SMEM, HBM, VMEM, VMEM, VMEM, VMEM),
        out_specs=specs(HBM, VMEM),
        scratch_shapes=[
            pltpu.VMEM(outcomes.shape, BF16),
            pltpu.VMEM(projected, F32),
            pltpu.SemaphoreType.DMA((2,)),
        ],
        compiler_params=pltpu.CompilerParams(vmem_limit_bytes=24 << 20),
        name="middle_stage",
    )(core, in_hbm(outcomes), *weights, *back)


def last_stage(gram, projected):
    rank = projected.shape[1]
    return pl.pallas_call(
        last_kernel,
        out_shape=[jax.ShapeDtypeStruct(dim, F32) for dim in (projected.shape, (rank, rank))],
        in_specs=specs(VMEM, HBM),
        out_specs=specs(VMEM, VMEM),
        scratch_shapes=[pltpu.VMEM(projected.shape, F32), pltpu.SemaphoreType.DMA],
        compiler_params=pltpu.CompilerParams(vmem_limit_bytes=16 << 20),
        name="last_stage",
    )(gram, in_hbm(projected))


def block_sum(blocks):
    return pl.pallas_call(
        sum_kernel,
        out_shape=pltpu.VMEM(blocks.shape[1:], F32),
        in_specs=specs(VMEM),
        out_specs=pl.BlockSpec(memory_space=VMEM),
        name="block_sum",
    )(pltpu.with_memory_space_constraint(blocks, VMEM))


def swap(block):
    return lax.ppermute(block, C, [(0, 1), (1, 0)])


def exchange(blocks, axes):
    return lax.all_to_all(blocks, axes, split_axis=0, concat_axis=0, tiled=True)


def to_all(block, axes):
    copies = jnp.broadcast_to(block, (lax.axis_size(axes), *block.shape))
    return exchange(copies, axes)


def scattered_sum(part, axes):
    blocks = part.reshape(lax.axis_size(axes), -1, part.shape[-1])
    return exchange(blocks, axes).sum(axis=0)


def gathered(own, axes):
    return to_all(own, axes).reshape(-1, own.shape[-1])


def row_sums(mine, other):
    blocks = (mine + swap(other)).reshape(lax.axis_size(X), -1, mine.shape[-1])
    mine = block_sum(exchange(blocks, X))
    return scattered_sum(mine, (Z, Y))


def gram_sum(part):
    mine = scattered_sum(part, (X, C))
    mine = to_all(mine, Z).sum(axis=0)
    mine = to_all(mine, Y).sum(axis=0)
    return gathered(mine, (X, C))


def per_device(outcomes, sketch):
    rows_here, day_count = outcomes.shape
    unit_count = rows_here * lax.axis_size(EVERY)
    per_unit, per_day = 1 / math.sqrt(unit_count), 1 / math.sqrt(day_count)
    core = lax.axis_index(C).astype(jnp.int32).reshape(1)

    own = row_sums(*first_stage(core, outcomes, sketch))
    mine = gathered((own * per_unit).astype(BF16), (X, Z, Y))
    weights = (mine, swap(mine))
    own = row_sums(*back_stage(core, outcomes, weights, per_day))
    mine = gathered(gathered(own, (Z, Y)), X)
    scales = (per_unit, per_day, per_day / unit_count, 1 / unit_count)
    projected, gram = middle_stage(core, outcomes, weights, (mine, swap(mine)), scales)
    return tuple(last_stage(gram_sum(gram), projected))


def solution(mesh):
    finer = Mesh(
        mesh.devices.reshape(4, 2, mesh.shape["gy"], mesh.shape["gz"]), EVERY
    )
    return jax.shard_map(
        per_device,
        mesh=finer,
        in_specs=(P(EVERY, None), P(EVERY, None)),
        out_specs=(P(EVERY, None), P()),
        check_vma=False,
    )
```
